256 devices in a mesh: seq: 16 (over y, z_hi, core), mp: 16 (over z_lo, x).
Axes of the slice: x: 4, y: 4, z: 8 (z_hi: 2, z_lo: 4; z = z_hi * 4 + z_lo), core: 2. Of those that a mesh axis runs over, the one named last changes fastest.
Arguments:
- hidden_in: bfloat16 [2048, 2048], P('seq'), may hold values from -0.59765625 to 0.59765625
- input_gain: float32 [2048], replicated, may hold values from 0.25 to 1.75
- w_query: bfloat16 [2048, 2048], P(None, 'mp'), may hold values from -0.125 to 0.125
- key_value_weight: bfloat16 [2048, 4096], P(None, 'mp'), may hold values from -1 to 1, as said below
- query_gain: float32 [128], replicated, may hold values from 0.25 to 1.75
- key_gain: float32 [128], replicated, may hold values from 0.25 to 1.75
- w_out: bfloat16 [2048, 2048], P('mp'), may hold values from -0.125 to 0.125
- post_gain: float32 [2048], replicated, may hold values from 0.25 to 1.75
- w_gate: bfloat16 [2048, 6144], P(None, 'mp'), may hold values from -0.125 to 0.125
- w_up: bfloat16 [2048, 6144], P(None, 'mp'), may hold values from -0.125 to 0.125
- w_down: bfloat16 [6144, 2048], P('mp'), may hold values from -0.078125 to 0.078125
- prefix_slot_cache: bfloat16 [32, 256, 8, 256], P('seq'), may hold values from -240 to 240, as said below
- block_table: int32 [32], replicated, may hold values from 0 to 31, each once
- request_prefix: int32 [32], replicated, may hold values from 0 to 3
- suffix_lengths: int32 [32], replicated, may hold values from 1 to 256, 2048 in all
Outputs:
- hidden_out: bfloat16 [2048, 2048], P('seq', 'mp')
- suffix_key_values: bfloat16 [2048, 2048], P('seq', 'mp')
The draws below stay inside these ranges and needn't reach their ends.
Inputs may be any that keep to these rules, and one draw needn't show every extreme that they name: block_table[p * 8 + i] is the slot holding block i of prefix p; every slot appears once. `suffix_lengths`: the lengths add up to 2048 and the longest is exactly 256. `prefix_slot_cache`: per slot, position and key-value head: a key in the first 128 entries, a value in the last 128. `key_value_weight`: columns of key-value head k: 2 equal blocks of 256, starting at k * 2 * 2 * 128.
All inputs are finite; a program needn't handle non-finite values.
Results may differ from the reference program's by a relative error of at most 0.025.
The reference program's roundings to bfloat16 on the way count: a program that leaves them out, or rounds other values in their place, can miss the bound.
Values may be sent and summed in bfloat16 or wider, within the bound.
A program may use at most 64 MiB of HBM per device.

```python
import math
import jax
import jax.numpy as jnp
import numpy as np
from jax import lax

MODEL_WIDTH = 2048
QUERY_HEADS = 16
KEY_VALUE_HEADS = 8
HEAD_WIDTH = 128
FF = 6144
SEQUENCE_TOKENS = 128
BLK_DEV = 2
SLOT_POSITIONS = 256
N_PREFIX = 4
REPLICAS = 2
SUFFIX_TOKENS = 2048
CACHE_SLOTS = 32
BPP = 8
PREF = 2048
REQUESTS = 32
MOST = 256


def draw_prefix_slot_cache(key, part):
    first_key = jax.random.fold_in(key, 0)
    sampled_values = jnp.clip(jax.random.normal(first_key, (CACHE_SLOTS, SLOT_POSITIONS, KEY_VALUE_HEADS, 2 * HEAD_WIDTH), jnp.float32), -6.0, 6.0)
    return sampled_values.astype(jnp.bfloat16)


def draw_key_value_weight(key, part):
    base_key = jax.random.fold_in(key, 17)
    sampled_values = jnp.clip(jax.random.normal(base_key, (MODEL_WIDTH, KEY_VALUE_HEADS, 1, 2 * HEAD_WIDTH), jnp.float32), -6.0, 6.0)
    sampled_values = sampled_values * MODEL_WIDTH ** (-0.5)
    copies = jnp.broadcast_to(sampled_values, (MODEL_WIDTH, KEY_VALUE_HEADS, REPLICAS, 2 * HEAD_WIDTH))
    return copies.reshape(MODEL_WIDTH, REPLICAS * 2 * KEY_VALUE_HEADS * HEAD_WIDTH).astype(jnp.bfloat16)


def plant(values, stream_key, smallest, top_value):
    place = [jax.random.randint(jax.random.fold_in(stream_key, axis), (), 0, length) for axis, length in enumerate(values.shape)]
    widest = values.shape.index(max(values.shape))
    next_to = place[:widest] + [(place[widest] + 1) % values.shape[widest]] + place[widest + 1:]
    return values.at[tuple(place)].set(smallest).at[tuple(next_to)].set(top_value)


def levels(stream_key, dims, pieces, smallest, top_value):
    factor_of, own = 1.0, jax.random.fold_in(stream_key, 6)
    for dim, parts in pieces:
        steps = jnp.exp(jax.random.uniform(jax.random.fold_in(own, dim), (parts,), jnp.float32, smallest / len(pieces), top_value / len(pieces)))
        factor_of = factor_of * jnp.repeat(steps, dims[dim] // parts).reshape([-1 if axis == dim else 1 for axis in range(len(dims))])
    return factor_of


def cumulative_ranks(count, slope):
    weights = [(1 << 20) // math.isqrt(grade ** slope) + 1 for grade in range(1, count + 1)]
    spread = 1 + sum(weights) // (1 << 30)
    return np.cumsum(np.array([max(1, weight // spread) for weight in weights]))


def ranked(own_key, dims, count, skew):
    table = cumulative_ranks(count, skew)
    ticket = jax.random.randint(jax.random.fold_in(own_key, 1), dims, 0, int(table[count - 1]))
    rank = jnp.searchsorted(jnp.asarray(table, jnp.int32), ticket, side="right")
    return jax.random.permutation(jax.random.fold_in(own_key, 2), count)[rank].astype(jnp.int32)


def profile(count, total, limit, slope):
    portions = [(1 << 20) // math.isqrt(rank ** slope) + 1 for rank in range(2, count + 1)]
    rest, holding = total - limit - (count - 1), [1] * (count - 1)
    while rest > 0:
        candidates = [i for i in range(count - 1) if holding[i] < limit]
        whole, remaining = sum([portions[i] for i in candidates]), rest
        for i in candidates:
            extra = min(limit - holding[i], max(1, remaining * portions[i] // whole), rest)
            holding[i] = holding[i] + extra
            rest = rest - extra
    return np.array([limit] + holding)


def ragged_sizes(own_key, count, total, bound, slope):
    if count == 2:
        one = jax.random.randint(own_key, (), max(1, total - bound), min(bound, total - 1) + 1)
        return jnp.stack([one, total - one])
    lengths = jnp.asarray(profile(count, total, bound, slope), jnp.int32)
    pairs = (count - 1) // 2
    giver, taker = lengths[1:1 + 2 * pairs:2], lengths[2:2 + 2 * pairs:2]
    slack = jnp.minimum(giver - 1, bound - taker)
    moved = jax.random.randint(jax.random.fold_in(own_key, 1), (pairs,), 0, 1 << 20) % (slack + 1)
    lengths = lengths.at[1:1 + 2 * pairs:2].set(giver - moved).at[2:2 + 2 * pairs:2].set(taker + moved)
    return lengths[jax.random.permutation(jax.random.fold_in(own_key, 2), count)]


def gaussian(key, shape, spread, most, shards=(), kind=jnp.bfloat16):
    level = levels(key, shape, shards, -0.22, 0.18) if shards else 1.0
    entries = jax.random.normal(key, shape, jnp.float32) * spread * level
    return jnp.minimum(jnp.maximum(entries, -most), most).astype(kind)


def setup_inputs(seed: int = 0) -> dict:
    seeds = jax.random.split(jax.random.key(seed), 16)
    hidden_in = gaussian(seeds[0], (SUFFIX_TOKENS, MODEL_WIDTH), 0.1, 0.59765625, ((0, 16),))
    input_gain = jnp.clip(1.0 + 0.15 * jax.random.normal(seeds[1], (MODEL_WIDTH,), jnp.float32), 0.25, 1.75)
    w_query = gaussian(seeds[2], (MODEL_WIDTH, QUERY_HEADS * HEAD_WIDTH), MODEL_WIDTH ** -0.5, 0.125, ((1, 16),))
    key_value_weight = draw_key_value_weight(jax.random.fold_in(seeds[15], 71), 0)
    query_gain = jnp.clip(1.0 + 0.15 * jax.random.normal(seeds[4], (HEAD_WIDTH,), jnp.float32), 0.25, 1.75)
    key_gain = jnp.clip(1.0 + 0.15 * jax.random.normal(seeds[5], (HEAD_WIDTH,), jnp.float32), 0.25, 1.75)
    w_out = gaussian(seeds[6], (QUERY_HEADS * HEAD_WIDTH, MODEL_WIDTH), (QUERY_HEADS * HEAD_WIDTH) ** -0.5, 0.125, ((0, 16),))
    post_gain = jnp.clip(1.0 + 0.15 * jax.random.normal(seeds[7], (MODEL_WIDTH,), jnp.float32), 0.25, 1.75)
    w_gate = gaussian(seeds[8], (MODEL_WIDTH, FF), MODEL_WIDTH ** -0.5, 0.125, ((1, 16),))
    w_up = gaussian(seeds[9], (MODEL_WIDTH, FF), MODEL_WIDTH ** -0.5, 0.125, ((1, 16),))
    w_down = gaussian(seeds[10], (FF, MODEL_WIDTH), FF ** -0.5, 0.078125, ((0, 16),))
    prefix_slot_cache = draw_prefix_slot_cache(jax.random.fold_in(seeds[15], 71), 0)
    block_table = jax.random.permutation(seeds[12], CACHE_SLOTS).astype(jnp.int32)
    request_prefix = plant(ranked(seeds[13], (REQUESTS,), N_PREFIX, 2), jax.random.fold_in(seeds[13], 3), 0, N_PREFIX - 1).astype(jnp.int32)
    suffix_lengths = ragged_sizes(seeds[14], REQUESTS, SUFFIX_TOKENS, MOST, 2).astype(jnp.int32)
    return dict(hidden_in=hidden_in, input_gain=input_gain, w_query=w_query, key_value_weight=key_value_weight, query_gain=query_gain, key_gain=key_gain, w_out=w_out, post_gain=post_gain, w_gate=w_gate, w_up=w_up, w_down=w_down, prefix_slot_cache=prefix_slot_cache, block_table=block_table, request_prefix=request_prefix, suffix_lengths=suffix_lengths)


EPSILON = 1e-06
THETA = 1000000.0
NEGATIVE_FLOOR = -1e+30

def token_tables(request_prefix, suffix_lengths, positions, prefix_length):
    request_ends = jnp.cumsum(suffix_lengths).astype(jnp.int32)
    starts = (request_ends - suffix_lengths).astype(jnp.int32)
    inside = ((positions[:, None] >= starts[None, :]) & (positions[:, None] < request_ends[None, :])).astype(jnp.int32)
    request_ids = jnp.arange(suffix_lengths.shape[0], dtype=jnp.int32)
    request_of = lax.optimization_barrier(jnp.sum(inside * request_ids[None, :], axis=1)).astype(jnp.int32)
    start_of = lax.optimization_barrier(jnp.sum(inside * starts[None, :], axis=1)).astype(jnp.int32)
    prefix_of = lax.optimization_barrier(jnp.sum(inside * request_prefix[None, :], axis=1)).astype(jnp.int32)
    rotary_pos = (prefix_length + positions - start_of).astype(jnp.int32)
    return (request_of, prefix_of, rotary_pos)

def row_norm(values, gain):
    return values * lax.rsqrt(lax.optimization_barrier(jnp.mean(values * values, axis=-1, keepdims=True)) + EPSILON) * gain

def head_norm(values, gain):
    return values * lax.rsqrt(lax.optimization_barrier(jnp.mean(values * values, axis=-1, keepdims=True)) + EPSILON) * gain

def rotate(values, rotary_pos):
    half_dim = values.shape[-1] // 2
    freq_ids = jnp.arange(half_dim).astype(jnp.float32)
    inverse = jnp.exp(freq_ids * (-2.0 * math.log(THETA) / values.shape[-1]))
    angles = rotary_pos.astype(jnp.float32)[:, None] * inverse[None, :]
    cosine = jnp.cos(angles)[:, None, :]
    sine_part = jnp.sin(angles)[:, None, :]
    first_half = values[..., :half_dim]
    second_half = values[..., half_dim:]
    return jnp.concatenate([first_half * cosine - second_half * sine_part, second_half * cosine + first_half * sine_part], axis=-1)

def allowed_keys(query_req, query_pre, query_pos, key_pre, key_req, key_pos):
    same_prefix = key_pre[None, :] == query_pre[:, None]
    same_request = (key_req[None, :] == query_req[:, None]) & (key_pos[None, :] <= query_pos[:, None])
    return same_prefix | same_request

def group_partial(query_rows_all, allowed, key_row_block, value_row_block):
    scaling = 1.0 / math.sqrt(query_rows_all.shape[-1])
    scores = jnp.einsum('nkgd,mkd->nkgm', query_rows_all.astype(jnp.float32), key_row_block.astype(jnp.float32)) * scaling
    allowed_full = allowed[:, None, None, :]
    scores = jnp.where(allowed_full, scores, NEGATIVE_FLOOR)
    highest_score = lax.optimization_barrier(jnp.max(scores, axis=-1))
    weights = jnp.where(allowed_full, jnp.exp(scores - highest_score[..., None]), 0.0)
    total_weight = lax.optimization_barrier(jnp.sum(weights, axis=-1))
    rounded = lax.optimization_barrier(weights.astype(jnp.bfloat16)).astype(jnp.float32)
    summed = jnp.einsum('nkgm,mkd->nkgd', rounded, value_row_block.astype(jnp.float32))
    layer_output = (summed / jnp.maximum(total_weight, 1.0)[..., None]).astype(jnp.bfloat16)
    return (highest_score, total_weight, layer_output)

def merge_group(running, highest_score, total_weight, layer_output):
    best_score, weight_sum, accumulated = running
    new_best = jnp.maximum(best_score, highest_score)
    old_factor = jnp.exp(best_score - new_best)
    new_factor = total_weight * jnp.exp(highest_score - new_best)
    return (new_best, weight_sum * old_factor + new_factor, accumulated * old_factor[..., None] + new_factor[..., None] * layer_output.astype(jnp.float32))

def reference(hidden_in, input_gain, w_query, key_value_weight, query_gain, key_gain, w_out, post_gain, w_gate, w_up, w_down, prefix_slot_cache, block_table, request_prefix, suffix_lengths):
    group_width = QUERY_HEADS // KEY_VALUE_HEADS
    hidden_f32 = hidden_in.astype(jnp.float32)
    normed = row_norm(hidden_f32, input_gain).astype(jnp.bfloat16)
    positions = jnp.arange(SUFFIX_TOKENS, dtype=jnp.int32)
    request_of, prefix_of, rotary_pos = token_tables(request_prefix, suffix_lengths, positions, PREF)
    query_raw = jnp.dot(normed, w_query, preferred_element_type=jnp.float32).reshape(SUFFIX_TOKENS, QUERY_HEADS, HEAD_WIDTH)
    query_rows_all = rotate(head_norm(query_raw, query_gain), rotary_pos).astype(jnp.bfloat16)
    query_rows_all = query_rows_all.reshape(SUFFIX_TOKENS, KEY_VALUE_HEADS, group_width, HEAD_WIDTH)
    first_copy = key_value_weight.reshape(MODEL_WIDTH, KEY_VALUE_HEADS, REPLICAS, 2 * HEAD_WIDTH)[:, :, 0, :].reshape(MODEL_WIDTH, 2 * KEY_VALUE_HEADS * HEAD_WIDTH)
    unscaled_pairs = jnp.dot(normed, first_copy, preferred_element_type=jnp.float32).astype(jnp.bfloat16)
    unscaled_pairs = unscaled_pairs.reshape(SUFFIX_TOKENS, KEY_VALUE_HEADS, 2, HEAD_WIDTH)
    key_row_block = rotate(head_norm(unscaled_pairs[:, :, 0].astype(jnp.float32), key_gain), rotary_pos).astype(jnp.bfloat16)
    value_row_block = unscaled_pairs[:, :, 1]
    suffix_key_values = jnp.stack([key_row_block, value_row_block], axis=2).reshape(SUFFIX_TOKENS, 2 * KEY_VALUE_HEADS * HEAD_WIDTH)
    slot_ids = jnp.arange(CACHE_SLOTS, dtype=jnp.int32)
    owner_hits = (block_table[:, None] == slot_ids[None, :]).astype(jnp.int32)
    slot_prefix = lax.optimization_barrier(jnp.sum(owner_hits * (slot_ids // BPP)[:, None], axis=0)).astype(jnp.int32)
    group_list = SUFFIX_TOKENS // SEQUENCE_TOKENS
    cache_extent = BLK_DEV * SLOT_POSITIONS
    grouped_cache = prefix_slot_cache.reshape(group_list, cache_extent, KEY_VALUE_HEADS, 2 * HEAD_WIDTH)
    grouped_keys = key_row_block.reshape(group_list, SEQUENCE_TOKENS, KEY_VALUE_HEADS, HEAD_WIDTH)
    grouped_values = value_row_block.reshape(group_list, SEQUENCE_TOKENS, KEY_VALUE_HEADS, HEAD_WIDTH)
    pre_groups = jnp.repeat(slot_prefix, SLOT_POSITIONS).reshape(group_list, cache_extent)
    req_groups = request_of.reshape(group_list, SEQUENCE_TOKENS)
    pos_groups = positions.reshape(group_list, SEQUENCE_TOKENS)
    tiled_queries = query_rows_all.reshape(group_list, SEQUENCE_TOKENS, KEY_VALUE_HEADS, group_width, HEAD_WIDTH)
    prefix_tiles = prefix_of.reshape(group_list, SEQUENCE_TOKENS)

    def one_group(running, members):
        cache_rows, group_keys, group_values, group_pre, group_req, group_pos = members
        all_keys = jnp.concatenate([cache_rows[..., :HEAD_WIDTH], group_keys], axis=0)
        all_values = jnp.concatenate([cache_rows[..., HEAD_WIDTH:], group_values], axis=0)
        key_pre = jnp.concatenate([group_pre, jnp.full((SEQUENCE_TOKENS,), -1, jnp.int32)])
        key_req = jnp.concatenate([jnp.full((cache_extent,), -1, jnp.int32), group_req])
        key_pos = jnp.concatenate([jnp.zeros((cache_extent,), jnp.int32), group_pos])

        def one_tile(tile_members):
            tile_queries, tile_req, tile_pre, tile_pos = tile_members
            allowed = allowed_keys(tile_req, tile_pre, tile_pos, key_pre, key_req, key_pos)
            return group_partial(tile_queries, allowed, all_keys, all_values)
        highest_score, total_weight, layer_output = lax.map(one_tile, (tiled_queries, req_groups, prefix_tiles, pos_groups))
        highest_score = highest_score.reshape(SUFFIX_TOKENS, KEY_VALUE_HEADS, group_width)
        total_weight = total_weight.reshape(SUFFIX_TOKENS, KEY_VALUE_HEADS, group_width)
        layer_output = layer_output.reshape(SUFFIX_TOKENS, KEY_VALUE_HEADS, group_width, HEAD_WIDTH)
        return (merge_group(running, highest_score, total_weight, layer_output), None)
    starting_carry = (jnp.full((SUFFIX_TOKENS, KEY_VALUE_HEADS, group_width), NEGATIVE_FLOOR, jnp.float32), jnp.zeros((SUFFIX_TOKENS, KEY_VALUE_HEADS, group_width), jnp.float32), jnp.zeros((SUFFIX_TOKENS, KEY_VALUE_HEADS, group_width, HEAD_WIDTH), jnp.float32))
    running, _ = lax.scan(one_group, starting_carry, (grouped_cache, grouped_keys, grouped_values, pre_groups, req_groups, pos_groups))
    best_score, weight_sum, accumulated = running
    attended = (accumulated / weight_sum[..., None]).astype(jnp.bfloat16).reshape(SUFFIX_TOKENS, QUERY_HEADS * HEAD_WIDTH)
    residual = (hidden_f32 + jnp.dot(attended, w_out, preferred_element_type=jnp.float32)).astype(jnp.bfloat16)
    post_normed = row_norm(residual.astype(jnp.float32), post_gain).astype(jnp.bfloat16)
    gate_terms = jnp.dot(post_normed, w_gate, preferred_element_type=jnp.float32)
    up_terms = jnp.dot(post_normed, w_up, preferred_element_type=jnp.float32)
    middle = (jax.nn.silu(gate_terms) * up_terms).astype(jnp.bfloat16)
    hidden_out = (residual.astype(jnp.float32) + jnp.dot(middle, w_down, preferred_element_type=jnp.float32)).astype(jnp.bfloat16)
    return (hidden_out, suffix_key_values)
```

```python
import functools
import math

import jax
import jax.numpy as jnp
from jax import lax
from jax.experimental import pallas as pl
from jax.experimental.pallas import tpu as pltpu
from jax.sharding import PartitionSpec as P

HEAD = 128
N_PREFIX = 4
EPSILON = 1e-06
THETA = 1000000.0
FLOOR = -1e30
MESH = pl.DeviceIdType.MESH
F32 = jnp.float32
BF16 = jnp.bfloat16


def push(src, dst, send_sem, recv_sem, axis, peer):
    return pltpu.make_async_remote_copy(
        src_ref=src,
        dst_ref=dst,
        send_sem=send_sem,
        recv_sem=recv_sem,
        device_id={axis: peer},
        device_id_type=MESH,
    )


def greet(axis, count, me):
    barrier = pltpu.get_barrier_semaphore()

    def one(step, carry):
        pl.semaphore_signal(
            barrier, inc=1, device_id={axis: lax.rem(me + step, count)}, device_id_type=MESH
        )
        return carry

    lax.fori_loop(1, count, one, 0)
    return barrier


def normalize(values, gain):
    return values * lax.rsqrt(jnp.mean(values * values, axis=-1, keepdims=True) + EPSILON) * gain


def attn_kernel(
    count,
    hidden_ref,
    gain_ref,
    wq_ref,
    wkv_ref,
    qgain_ref,
    kgain_ref,
    cos_ref,
    sin_ref,
    cache_ref,
    table_ref,
    prefix_ref,
    length_ref,
    att_ref,
    skv_ref,
    q_all,
    keys,
    values_t,
    out_send,
    stat_send,
    out_recv,
    stat_recv,
    q_send_sem,
    q_recv_sem,
    o_send_sem,
    o_recv_sem,
    s_send_sem,
    s_recv_sem,
):
    me = lax.axis_index("seq")
    my_model = lax.axis_index("mp")
    rows = hidden_ref.shape[0]
    cached = cache_ref.shape[0]
    slot_rows = cached // 2
    barrier = greet("seq", count, me)

    normed = normalize(hidden_ref[...].astype(F32), gain_ref[...]).astype(BF16)
    cosine, sine = cos_ref[...], sin_ref[...]

    def rope(x):
        return x * cosine + pltpu.roll(x, HEAD // 2, 1) * sine

    q_raw = jnp.dot(normed, wq_ref[...], preferred_element_type=F32)
    q_all[me] = rope(normalize(q_raw, qgain_ref[...])).astype(BF16)
    pl.semaphore_wait(barrier, count - 1)

    def send_q(step, carry):
        peer = lax.rem(me + step, count)
        push(
            q_all.at[me], q_all.at[me], q_send_sem.at[peer], q_recv_sem.at[me], "seq", peer
        ).start()
        return carry

    lax.fori_loop(1, count, send_q, 0)

    pair = jnp.dot(normed, wkv_ref[...], preferred_element_type=F32).astype(BF16)
    key = rope(normalize(pair[:, :HEAD].astype(F32), kgain_ref[...])).astype(BF16)
    value = pair[:, HEAD:]
    skv_ref[...] = jnp.where(lax.rem(my_model, 2) == 0, key.astype(F32), value.astype(F32)).astype(
        BF16
    )
    keys[pl.ds(0, cached), :] = cache_ref[:, :HEAD]
    keys[pl.ds(cached, rows), :] = key
    values_t[:, pl.ds(0, cached)] = cache_ref[:, HEAD:].astype(F32).T.astype(BF16)
    values_t[:, pl.ds(cached, rows)] = value.astype(F32).T.astype(BF16)

    requests = length_ref.shape[1]
    lengths = jnp.broadcast_to(length_ref[...], (requests, requests))
    row_id = lax.broadcasted_iota(jnp.int32, (requests, requests), 0)
    col_id = lax.broadcasted_iota(jnp.int32, (requests, requests), 1)
    ends = jnp.sum(jnp.where(col_id <= row_id, lengths, 0), axis=1, keepdims=True)
    starts = jnp.sum(jnp.where(col_id < row_id, lengths, 0), axis=1, keepdims=True)
    prefixes = prefix_ref[...]
    table = table_ref[...]
    slots = table.shape[1]
    owner = lax.broadcasted_iota(jnp.int32, (1, slots), 1) // (slots // N_PREFIX)
    slot_a = jnp.sum(jnp.where(table == 2 * me, owner, 0), axis=1, keepdims=True)
    slot_b = jnp.sum(jnp.where(table == 2 * me + 1, owner, 0), axis=1, keepdims=True)
    scale = 1.0 / math.sqrt(HEAD)

    def partial(chunk):
        position = chunk * rows + lax.broadcasted_iota(jnp.int32, (1, rows), 1)
        inside = (position >= starts) & (position < ends)
        start_of = jnp.sum(jnp.where(inside, starts, 0), axis=0, keepdims=True)
        prefix_of = jnp.sum(jnp.where(inside, prefixes, 0), axis=0, keepdims=True)
        score = (
            lax.dot_general(
                keys[...], q_all[chunk], (((1,), (1,)), ((), ())), preferred_element_type=F32
            )
            * scale
        )
        key_pos = me * rows + lax.broadcasted_iota(jnp.int32, (rows, rows), 0)
        score_a = jnp.where(prefix_of == slot_a, score[:slot_rows], FLOOR)
        score_b = jnp.where(prefix_of == slot_b, score[slot_rows:cached], FLOOR)
        score_c = jnp.where((key_pos >= start_of) & (key_pos <= position), score[cached:], FLOOR)
        score = jnp.concatenate([score_a, score_b, score_c], axis=0)
        peak = jnp.max(score, axis=0, keepdims=True)
        weight = jnp.exp(score - jnp.where(peak < 0.1 * FLOOR, 0.0, peak))
        total = jnp.sum(weight, axis=0, keepdims=True)
        out = jnp.dot(values_t[...], weight.astype(BF16), preferred_element_type=F32)
        out = (out / jnp.maximum(total, 1.0)).astype(BF16)
        stats = jnp.concatenate(
            [jnp.broadcast_to(peak, (4, rows)), jnp.broadcast_to(total, (4, rows))], axis=0
        )
        return out, stats

    own_out, own_stats = partial(me)
    out_recv[me] = own_out
    stat_recv[me] = own_stats

    def answer(step, carry):
        peer = lax.rem(me + count - step, count)
        push(
            q_all.at[peer], q_all.at[peer], q_send_sem.at[peer], q_recv_sem.at[peer], "seq", peer
        ).wait_recv()
        out, stats = partial(peer)
        out_send[peer] = out
        stat_send[peer] = stats
        push(
            out_send.at[peer], out_recv.at[me], o_send_sem.at[peer], o_recv_sem.at[me], "seq", peer
        ).start()
        push(
            stat_send.at[peer],
            stat_recv.at[me],
            s_send_sem.at[peer],
            s_recv_sem.at[me],
            "seq",
            peer,
        ).start()
        return carry

    lax.fori_loop(1, count, answer, 0)

    def collect(step, carry):
        peer = lax.rem(me + step, count)
        push(
            out_send.at[peer], out_recv.at[peer], o_send_sem.at[peer], o_recv_sem.at[peer], "seq", peer
        ).wait()
        push(
            stat_send.at[peer],
            stat_recv.at[peer],
            s_send_sem.at[peer],
            s_recv_sem.at[peer],
            "seq",
            peer,
        ).wait()
        push(
            q_all.at[me], q_all.at[me], q_send_sem.at[peer], q_recv_sem.at[peer], "seq", peer
        ).wait_send()
        return carry

    lax.fori_loop(1, count, collect, 0)
    best = stat_recv[0, 0:1, :]
    for group in range(1, count):
        best = jnp.maximum(best, stat_recv[group, 0:1, :])
    below = jnp.zeros((1, rows), F32)
    above = jnp.zeros((HEAD, rows), F32)
    for group in range(count):
        factor = stat_recv[group, 4:5, :] * jnp.exp(stat_recv[group, 0:1, :] - best)
        below += factor
        above += factor * out_recv[group].astype(F32)
    att_ref[...] = (above / below).T.astype(BF16)


def ffn_kernel(
    count,
    att_ref,
    hidden_ref,
    wo_ref,
    gain_ref,
    wg_hbm,
    wu_hbm,
    wd_hbm,
    out_ref,
    wg,
    wu,
    wd,
    part_send,
    part_recv,
    residual,
    post,
    down_send,
    down_recv,
    w_sem,
    a_send_sem,
    a_recv_sem,
    r_send_sem,
    r_recv_sem,
    d_send_sem,
    d_recv_sem,
):
    me = lax.axis_index("mp")
    barrier = greet("mp", count, me)
    loads = [
        pltpu.make_async_copy(wg_hbm, wg, w_sem.at[0]),
        pltpu.make_async_copy(wu_hbm, wu, w_sem.at[1]),
        pltpu.make_async_copy(wd_hbm, wd, w_sem.at[2]),
    ]
    for load in loads:
        load.start()
    width = HEAD

    def columns(chunk):
        return pl.ds(pl.multiple_of(chunk * width, width), width)

    att = att_ref[...]
    pl.semaphore_wait(barrier, count - 1)

    def send_part(step, carry):
        peer = lax.rem(me + step, count)
        part_send[peer] = jnp.dot(
            att, wo_ref[:, columns(peer)], preferred_element_type=F32
        ).astype(BF16)
        push(
            part_send.at[peer], part_recv.at[me], a_send_sem.at[peer], a_recv_sem.at[me], "mp", peer
        ).start()
        return carry

    lax.fori_loop(1, count, send_part, 0)
    mine = jnp.dot(att, wo_ref[:, columns(me)], preferred_element_type=F32)

    def add_part(step, total):
        peer = lax.rem(me + count - step, count)
        push(
            part_send.at[peer], part_recv.at[peer], a_send_sem.at[peer], a_recv_sem.at[peer], "mp", peer
        ).wait()
        return total + part_recv[peer].astype(F32)

    mine = lax.fori_loop(1, count, add_part, mine)
    residual[me] = (hidden_ref[:, columns(me)].astype(F32) + mine).astype(BF16)

    def send_residual(step, carry):
        peer = lax.rem(me + step, count)
        push(
            residual.at[me], residual.at[me], r_send_sem.at[peer], r_recv_sem.at[me], "mp", peer
        ).start()
        return carry

    lax.fori_loop(1, count, send_residual, 0)

    def take_residual(step, carry):
        peer = lax.rem(me + count - step, count)
        push(
            residual.at[peer], residual.at[peer], r_send_sem.at[peer], r_recv_sem.at[peer], "mp", peer
        ).wait()
        return carry

    lax.fori_loop(1, count, take_residual, 0)
    squares = jnp.zeros((residual.shape[1], width), F32)
    for chunk in range(count):
        values = residual[chunk].astype(F32)
        squares += values * values
    inverse = lax.rsqrt(jnp.sum(squares, axis=1, keepdims=True) * (1.0 / (count * width)) + EPSILON)
    for chunk in range(count):
        span = pl.ds(chunk * width, width)
        post[:, span] = (residual[chunk].astype(F32) * inverse * gain_ref[:, span]).astype(BF16)
    loads[0].wait()
    gate = jnp.dot(post[...], wg[...], preferred_element_type=F32)
    loads[1].wait()
    up = jnp.dot(post[...], wu[...], preferred_element_type=F32)
    middle = (gate / (1.0 + jnp.exp(-gate)) * up).astype(BF16)
    loads[2].wait()

    def send_down(step, carry):
        peer = lax.rem(me + step, count)
        down_send[peer] = jnp.dot(
            middle, wd[:, columns(peer)], preferred_element_type=F32
        ).astype(BF16)
        push(
            down_send.at[peer], down_recv.at[me], d_send_sem.at[peer], d_recv_sem.at[me], "mp", peer
        ).start()
        return carry

    lax.fori_loop(1, count, send_down, 0)
    total = jnp.dot(middle, wd[:, columns(me)], preferred_element_type=F32)

    def add_down(step, total):
        peer = lax.rem(me + count - step, count)
        push(
            down_send.at[peer], down_recv.at[peer], d_send_sem.at[peer], d_recv_sem.at[peer], "mp", peer
        ).wait()
        return total + down_recv[peer].astype(F32)

    total = lax.fori_loop(1, count, add_down, total)
    out_ref[...] = (residual[me].astype(F32) + total).astype(BF16)


def local(
    hidden_in,
    input_gain,
    w_query,
    key_value_weight,
    query_gain,
    key_gain,
    w_out,
    post_gain,
    w_gate,
    w_up,
    w_down,
    prefix_slot_cache,
    block_table,
    request_prefix,
    suffix_lengths,
):
    seq_count = lax.axis_size("seq")
    model_count = lax.axis_size("mp")
    my_seq = lax.axis_index("seq")
    my_model = lax.axis_index("mp")
    rows, model = hidden_in.shape
    slots, slot_rows, kv_heads, pair_width = prefix_slot_cache.shape
    prefix_length = slots * seq_count // N_PREFIX * slot_rows
    cache_mine = lax.dynamic_slice_in_dim(
        prefix_slot_cache, my_model * kv_heads // model_count, 1, 2
    ).reshape(slots * slot_rows, pair_width)

    positions = my_seq * rows + jnp.arange(rows, dtype=jnp.int32)
    request_ends = jnp.cumsum(suffix_lengths)
    starts = request_ends - suffix_lengths
    inside = (positions[:, None] >= starts[None, :]) & (positions[:, None] < request_ends[None, :])
    start_of = jnp.sum(jnp.where(inside, starts[None, :], 0), axis=1)
    rotary_pos = (prefix_length + positions - start_of).astype(F32)
    half = HEAD // 2
    inverse = jnp.exp(jnp.arange(half).astype(F32) * (-2.0 * math.log(THETA) / HEAD))
    angles = rotary_pos[:, None] * inverse[None, :]
    cosine, sine = jnp.cos(angles), jnp.sin(angles)
    cosine = jnp.concatenate([cosine, cosine], axis=1)
    sine = jnp.concatenate([-sine, sine], axis=1)

    vmem = pl.BlockSpec(memory_space=pltpu.VMEM)
    anywhere = pl.BlockSpec(memory_space=pl.ANY)
    dma = pltpu.SemaphoreType.DMA
    block = jax.ShapeDtypeStruct((rows, HEAD), BF16)
    attended, suffix_key_values = pl.pallas_call(
        functools.partial(attn_kernel, seq_count),
        out_shape=(block, block),
        in_specs=[vmem] * 12,
        out_specs=(vmem, vmem),
        scratch_shapes=[
            pltpu.VMEM((seq_count, rows, HEAD), BF16),
            pltpu.VMEM((slots * slot_rows + rows, HEAD), BF16),
            pltpu.VMEM((HEAD, slots * slot_rows + rows), BF16),
            pltpu.VMEM((seq_count, HEAD, rows), BF16),
            pltpu.VMEM((seq_count, 8, rows), F32),
            pltpu.VMEM((seq_count, HEAD, rows), BF16),
            pltpu.VMEM((seq_count, 8, rows), F32),
        ]
        + [dma((seq_count,))] * 6,
        compiler_params=pltpu.CompilerParams(collective_id=0, has_side_effects=True),
        name="attn",
    )(
        hidden_in,
        input_gain.reshape(1, model),
        w_query,
        key_value_weight,
        query_gain.reshape(1, HEAD),
        key_gain.reshape(1, HEAD),
        cosine,
        sine,
        cache_mine,
        block_table.reshape(1, -1),
        request_prefix.reshape(-1, 1),
        suffix_lengths.reshape(1, -1),
    )
    column_block = (model_count, rows, model // model_count)
    hidden_out = pl.pallas_call(
        functools.partial(ffn_kernel, model_count),
        out_shape=block,
        in_specs=[vmem] * 4 + [anywhere] * 3,
        out_specs=vmem,
        scratch_shapes=[
            pltpu.VMEM(w_gate.shape, BF16),
            pltpu.VMEM(w_up.shape, BF16),
            pltpu.VMEM(w_down.shape, BF16),
            pltpu.VMEM(column_block, BF16),
            pltpu.VMEM(column_block, BF16),
            pltpu.VMEM(column_block, BF16),
            pltpu.VMEM((rows, model), BF16),
            pltpu.VMEM(column_block, BF16),
            pltpu.VMEM(column_block, BF16),
            dma((3,)),
        ]
        + [dma((model_count,))] * 6,
        compiler_params=pltpu.CompilerParams(collective_id=1, has_side_effects=True),
        name="ffn",
    )(
        attended,
        hidden_in,
        w_out,
        post_gain.reshape(1, model),
        w_gate,
        w_up,
        w_down,
    )
    return (hidden_out, suffix_key_values)


def solution(mesh):
    in_specs = (
        P("seq", None),
        P(),
        P(None, "mp"),
        P(None, "mp"),
        P(),
        P(),
        P("mp", None),
        P(),
        P(None, "mp"),
        P(None, "mp"),
        P("mp", None),
        P("seq", None, None, None),
        P(),
        P(),
        P(),
    )
    out_specs = (P("seq", "mp"), P("seq", "mp"))
    return jax.shard_map(local, mesh=mesh, in_specs=in_specs, out_specs=out_specs, check_vma=False)
```
